512 devices in a mesh: space: 16 (over x_hi, y, core), tm: 32 (over z, x_lo).
Axes of the slice: x: 4 (x_hi: 2, x_lo: 2; x = x_hi * 2 + x_lo), y: 4, z: 16, core: 2. Of those that a mesh axis runs over, the one named last changes fastest.
Arguments:
- space_factor: bfloat16 [64, 65536], P('tm', 'space'), may hold values from -2.5 to 2.5
- time_factor: bfloat16 [64, 8192], P('space', 'tm'), may hold values from -2.5 to 2.5
- initial_state: float32 [65536], P('space'), may hold values from -6 to 6
- link: int32 [65536], P('space'), may hold values from 1 to 4
- conductivity: float32 [65536], P('space'), may hold values from 0.2 to 2
- mass: float32 [65536], P('space'), may hold values from 0.5 to 2
- reaction: float32 [65536], P('space'), may hold values from 0.05 to 0.4
- source: bfloat16 [65536, 8192], P('space', 'tm'), may hold values from -6 to 6
Outputs:
- grad_space: float32 [64, 65536], P('tm', 'space')
- grad_time: float32 [64, 8192], P('space', 'tm')
The draws below stay inside these ranges and needn't reach their ends.
Inputs may be any that keep to these rules, and one draw needn't show every extreme that they name: Element i joins node i and node i + link[i]; where that node lies past the last node, the element ties node i to a zero value.
All inputs are finite; a program needn't handle non-finite values.
Results may differ from the reference program's by a relative error of at most 0.00055.
Values may be sent and summed in bfloat16 or wider, within the bound.
No kernel may reach another device: no remote copies, remote signals or barrier semaphores. Data moves between devices by JAX's collectives and lax.ppermute only.
A program may use at most 64 MiB of HBM per device.

```python
import math
import jax
import jax.numpy as jnp
from jax import lax

R = 64
W = 4
STEP_DEV = 256
NODES = 65536
STEPS = 8192
N_TM = 32


def plant(values, key, low, largest):
    spot = [jax.random.randint(jax.random.fold_in(key, axis), (), 0, length) for axis, length in enumerate(values.shape)]
    widest = values.shape.index(max(values.shape))
    neighbour = spot[:widest] + [(spot[widest] + 1) % values.shape[widest]] + spot[widest + 1:]
    return values.at[tuple(spot)].set(low).at[tuple(neighbour)].set(largest)


def block_levels(own_key, extent, cuts, least, high):
    gain = 1.0
    for axis_at, parts in cuts:
        steps = jax.random.uniform(jax.random.fold_in(jax.random.fold_in(own_key, 6), axis_at), (parts,), jnp.float32, least / len(cuts), high / len(cuts))
        gain = gain * jnp.repeat(jnp.exp(steps), extent[axis_at] // parts).reshape((-1,) + (1,) * (len(extent) - 1 - axis_at))
    return gain


def gaussian(own_key, extent, width, limit, cuts=(), kind=jnp.bfloat16):
    array = jax.random.normal(own_key, extent, jnp.float32) * width
    if len(cuts) > 0:
        array = block_levels(own_key, extent, cuts, -0.22, 0.18) * array
    return jnp.clip(array, min=-limit, max=limit).astype(kind)


def setup_inputs(seed: int = 0) -> dict:
    arg_keys = jax.random.split(jax.random.key(seed), 9)
    space_factor = gaussian(arg_keys[0], (R, NODES), 0.35, 2.5, ((0, 32), (1, 16)))
    time_factor = gaussian(arg_keys[1], (R, STEPS), 0.35, 2.5, ((0, 16), (1, 32)))
    initial_state = gaussian(arg_keys[2], (NODES,), 1.0, 6.0, ((0, 16),), jnp.float32)
    link = plant(jax.random.randint(arg_keys[3], (NODES,), 1, W + 1), jax.random.fold_in(arg_keys[3], 1), 1, W).astype(jnp.int32)
    conductivity = jnp.clip(jnp.exp(math.log(2.0) - 2.3025851 * jax.random.uniform(arg_keys[4], (NODES,), jnp.float32) ** block_levels(arg_keys[4], (NODES,), ((0, 16),), -0.2, 0.2)), 0.2, 2.0)
    mass = jnp.clip(jnp.exp(math.log(2.0) - 1.3862944 * jax.random.uniform(arg_keys[5], (NODES,), jnp.float32) ** block_levels(arg_keys[5], (NODES,), ((0, 16),), -0.2, 0.2)), 0.5, 2.0)
    reaction = jnp.clip(jnp.exp(math.log(0.4) - 2.0794415 * jax.random.uniform(arg_keys[6], (NODES,), jnp.float32) ** block_levels(arg_keys[6], (NODES,), ((0, 16),), -0.2, 0.2)), 0.05, 0.4)
    source = gaussian(arg_keys[7], (NODES, STEPS), 1.0, 6.0, ((0, 16), (1, 32)))
    return dict(space_factor=space_factor, time_factor=time_factor, initial_state=initial_state, link=link, conductivity=conductivity, mass=mass, reaction=reaction, source=source)


def diffuse(padded, rates_padded, count):
    total = None
    for offset in range(1, W + 1):
        own_rate = rates_padded[offset - 1, W:W + count][:, None]
        came_rate = rates_padded[offset - 1, W - offset:W - offset + count][:, None]
        centre = padded[W:W + count]
        term = own_rate * (centre - padded[W + offset:W + offset + count]) - came_rate * (padded[W - offset:W - offset + count] - centre)
        total = term if total is None else total + term
    return total

def reference(space_factor, time_factor, initial_state, link, conductivity, mass, reaction, source):
    offsets = jnp.arange(1, W + 1, dtype=jnp.int32)[:, None]
    rates = jnp.where(link[None, :] == offsets, conductivity[None, :], 0.0)
    rates_padded = jnp.pad(rates, ((0, 0), (W, W)))
    zero_col = jnp.zeros((R, 1), time_factor.dtype)
    time_padded = jnp.concatenate([zero_col, time_factor, zero_col], axis=1)
    source_padded = jnp.concatenate([source, jnp.zeros((NODES, 1), source.dtype)], axis=1)
    space_t = space_factor.T
    mass_col = mass[:, None]
    react_col = reaction[:, None]

    def advance(accum, block):
        begin = block * STEP_DEV
        window = lax.dynamic_slice_in_dim(time_padded, begin, STEP_DEV + 2, 1)
        extended = jnp.dot(space_t, window, preferred_element_type=jnp.float32)
        prior_col = jnp.where(block == 0, initial_state, extended[:, 0])
        state = extended[:, 1:]
        earlier = jnp.concatenate([prior_col[:, None], extended[:, 1:-1]], axis=1)
        forcing = lax.dynamic_slice_in_dim(source_padded, begin, STEP_DEV + 1, 1).astype(jnp.float32)
        padded = jnp.pad(state, ((W, W), (0, 0)))
        residual = mass_col * (state - earlier) + diffuse(padded, rates_padded, NODES) + react_col * state * state * state - forcing
        inside = jnp.arange(STEP_DEV, dtype=jnp.int32) + begin + 1 < STEPS
        current = residual[:, :STEP_DEV]
        later = jnp.where(inside[None, :], residual[:, 1:], 0.0)
        present = state[:, :STEP_DEV]
        descent = mass_col * (current - later) + diffuse(jnp.pad(current, ((W, W), (0, 0))), rates_padded, NODES) + 3.0 * react_col * present * present * current
        descent_b = descent.astype(jnp.bfloat16)
        own_steps = lax.dynamic_slice_in_dim(time_factor, begin, STEP_DEV, 1)
        accum = accum + lax.dot_general(own_steps, descent_b, (((1,), (1,)), ((), ())), preferred_element_type=jnp.float32)
        block_grad = jnp.dot(space_factor, descent_b, preferred_element_type=jnp.float32)
        return (accum, block_grad)
    start_sum = jnp.zeros((R, NODES), jnp.float32)
    total, pieces = lax.scan(advance, start_sum, jnp.arange(N_TM, dtype=jnp.int32))
    grad_space = total / math.sqrt(STEPS)
    grad_time = jnp.transpose(pieces, (1, 0, 2)).reshape(R, STEPS) / math.sqrt(NODES)
    return (grad_space, grad_time)
```

```python
import functools
import math

import jax
import jax.numpy as jnp
from jax import lax
from jax.experimental import pallas as pl
from jax.experimental.pallas import tpu as pltpu
from jax.sharding import PartitionSpec as P


W = 4
PAD = 128
TILE = 256
UNROLL = 2
BF = jnp.bfloat16
F32 = jnp.float32


def dot(a, b, ca, cb):
    return lax.dot_general(a, b, (((ca,), (cb,)), ((), ())), preferred_element_type=F32)


def halves(x):
    hi = x.astype(BF)
    return hi, (x - hi.astype(F32)).astype(BF)


def pack_kernel(
    s_lo, s_hi, cond_lo, cond_hi, link_lo, link_hi, mass_lo, mass_hi, reac_lo, reac_hi,
    init_lo, init_hi, src_lo, src_hi, src_first, time_ref, up_ref, down_ref, prev_ref, next_ref,
):
    for ref, parts, src in (
        (down_ref, (s_lo, cond_lo, link_lo, mass_lo, reac_lo, init_lo), src_lo[0:4, :]),
        (up_ref, (s_hi, cond_hi, link_hi, mass_hi, reac_hi, init_hi), src_hi[12:16, :]),
    ):
        rows = [p[...].astype(F32) for p in parts]
        rows.append(jnp.zeros((1, PAD), F32))
        src = src.astype(F32)
        ref[...] = jnp.concatenate(rows + [src[:, 0:PAD], src[:, PAD:]], axis=0)

    nodes = src_first.shape[0]
    steps = time_ref.shape[1]
    row = lax.broadcasted_iota(jnp.int32, (16, steps), 0)
    col = lax.broadcasted_iota(jnp.int32, (16, steps), 1)
    pick = jnp.where(((row == 0) & (col == 0)) | ((row == 1) & (col == steps - 1)), 1.0, 0.0).astype(BF)
    column = dot(pick[:, 0:PAD], src_first[...], 1, 1)
    for c in range(nodes // PAD):
        prev_ref[c : c + 1, :] = column[0:1, c * PAD : (c + 1) * PAD]
    ends = dot(pick, time_ref[...], 1, 1)[0:8]
    ends = jnp.concatenate([ends, jnp.zeros((8, PAD - ends.shape[1]), F32)], axis=1)
    prev_ref[nodes // PAD :, :] = ends
    next_ref[...] = ends


def encode_kernel(own_ref, came_ref, out_ref, flat_ref):
    rows, nodes = own_ref.shape
    n_row = nodes // PAD
    n_z = out_ref.shape[0]
    own_rank = rows // n_z
    body = own_rank * n_row
    for g in range(rows // 8):
        v = own_ref[8 * g : 8 * g + 8, :] + came_ref[8 * g : 8 * g + 8, :]
        top = jnp.max(jnp.abs(v), axis=1, keepdims=True)
        power = jnp.ceil(jnp.log2(jnp.maximum(top, 1e-30)) + 0.01) - 15.0
        q = jnp.floor(v * jnp.exp2(-power) + 0.5)
        for c in range(n_row):
            flat_ref[pl.ds(8 * g * n_row + c, 8, stride=n_row), :] = q[:, c * PAD : (c + 1) * PAD]
        for b in range(8):
            z, at = divmod(8 * g + b, own_rank)
            flat_ref[rows * n_row + 8 * z + at : rows * n_row + 8 * z + at + 1, :] = jnp.broadcast_to(
                power[b : b + 1], (1, PAD)
            )
    for z in range(n_z):
        out_ref[z, 0:body, :] = flat_ref[z * body : (z + 1) * body, :].astype(jnp.int32).astype(jnp.int16)
        tail = flat_ref[rows * n_row + 8 * z : rows * n_row + 8 * z + 8, :]
        tail = jnp.where(lax.broadcasted_iota(jnp.int32, (8, PAD), 0) < own_rank, tail, 0.0)
        out_ref[z, body : body + 8, :] = tail.astype(jnp.int32).astype(jnp.int16)


def decode_kernel(factor, in_ref, out_ref):
    n_z = in_ref.shape[0]
    own_rank, nodes = out_ref.shape
    n_row = nodes // PAD
    body = own_rank * n_row
    total = jnp.zeros((body, PAD), F32)
    for z in range(n_z):
        step = jnp.exp2(in_ref[z, body : body + 8, :].astype(jnp.int32).astype(F32))
        q = in_ref[z, 0:body, :].astype(jnp.int32).astype(F32)
        total = total + jnp.concatenate(
            [q[b * n_row : (b + 1) * n_row] * step[b : b + 1] for b in range(own_rank)], axis=0
        )
    total = total * factor
    for b in range(own_rank):
        for c in range(n_row):
            out_ref[b : b + 1, c * PAD : (c + 1) * PAD] = total[b * n_row + c : b * n_row + c + 1]


def compute_kernel(
    flag_ref, sown_ref, soth_ref, tt_ref, qt_ref, tlast_ref,
    below_ref, above_ref, cond_ref, link_ref, mass_ref, reac_ref, init_ref, srcn_ref, src_ref, edge_ref,
    gs_own_ref, gs_oth_ref, gt_ref,
    w_ref, g_ref, coef_ref, band_ref, row_ref, sn_ref, rn_ref, y_ref, acc1_ref, acc2_ref, acc3_ref,
):
    ext = coef_ref.shape[1]
    nodes = ext - 2 * PAD
    rank = tlast_ref.shape[0]
    half = rank // 2
    steps = src_ref.shape[1]
    main = pl.ds(PAD, nodes)
    right = pl.ds(PAD + nodes, PAD)

    for r, ref in enumerate((cond_ref, link_ref, mass_ref, reac_ref, init_ref)):
        coef_ref[r : r + 1, 0:PAD] = below_ref[2 + r : 3 + r, :]
        coef_ref[r : r + 1, main] = ref[...].astype(F32)
        coef_ref[r : r + 1, right] = above_ref[2 + r : 3 + r, :]

    cond = coef_ref[0:1, :]
    link = coef_ref[1:2, :]
    mass = coef_ref[2:3, :]
    diag = mass + cond
    tall = (8, ext)
    for d in range(1, W + 1):
        up = jnp.where(link == float(d), cond, 0.0)
        down = pltpu.roll(up, d, 1)
        band_ref[8 * d : 8 * d + 8, :] = jnp.broadcast_to(up, tall)
        band_ref[8 * (W + d) : 8 * (W + d) + 8, :] = jnp.broadcast_to(down, tall)
        diag = diag + down
    band_ref[0:8, :] = jnp.broadcast_to(diag, tall)
    band_ref[8 * (2 * W + 1) : 8 * (2 * W + 2), :] = jnp.broadcast_to(mass, tall)
    start = flag_ref[0]
    coef_ref[4:5, :] = coef_ref[4:5, :] * mass * start

    n_tile = ext // PAD

    def place(c):
        k, h = (n_tile // 2 - 1, int(c > 0)) if c in (0, n_tile - 1) else divmod(c - 1, 2)
        return k, slice(h * PAD, (h + 1) * PAD)

    for c in range(n_tile):
        k, sl = place(c)
        row_ref[k, 0:2, sl] = coef_ref[3:5, c * PAD : (c + 1) * PAD]

    lane1 = lax.broadcasted_iota(jnp.int32, (8, PAD), 1)

    def banded(tiles, keep):
        fwd = [[pltpu.roll(x, PAD - d, 1) for d in range(1, W + 1)] for x in tiles]
        bwd = [[pltpu.roll(x, d, 1) for d in range(1, W + 1)] for x in tiles]
        for c in range(n_tile):
            sl = slice(c * PAD, (c + 1) * PAD)
            nxt, prv = min(c + 1, n_tile - 1), max(c - 1, 0)
            total = band_ref[0:8, sl] * tiles[c]
            for d in range(1, W + 1):
                ahead = jnp.where(lane1 >= PAD - d, fwd[nxt][d - 1], fwd[c][d - 1])
                back = jnp.where(lane1 < d, bwd[prv][d - 1], bwd[c][d - 1])
                total = total - band_ref[8 * d : 8 * d + 8, sl] * ahead
                total = total - band_ref[8 * (W + d) : 8 * (W + d) + 8, sl] * back
            keep(c, total, tiles[c])

    for base, ref in ((0, sown_ref), (half, soth_ref)):
        def fill(i, _, base=base, ref=ref):
            at = pl.multiple_of(i * 16, 16)
            to = pl.multiple_of(base + i * 16, 16)
            s_b = ref[pl.ds(at, 16), :]
            s_f = s_b.astype(F32)
            got = []
            for h in range(2):
                mine = {}

                def keep(c, value, v, mine=mine):
                    m = band_ref[8 * (2 * W + 1) : 8 * (2 * W + 2), c * PAD : (c + 1) * PAD]
                    if c in (0, n_tile - 1):
                        value = jnp.where(m > 0.0, value, 0.0)
                    mine[c] = (value, m * v)

                banded([s_f[8 * h : 8 * h + 8, c * PAD : (c + 1) * PAD] for c in range(n_tile)], keep)
                got.append(mine)
            for c in range(n_tile):
                k, sl = place(c)
                w_ref[k, pl.ds(to + 4 * rank, 16), sl] = s_b[:, c * PAD : (c + 1) * PAD]
                a_hi, a_lo = halves(jnp.concatenate([got[0][c][0], got[1][c][0]], axis=0))
                b_hi, b_lo = halves(jnp.concatenate([got[0][c][1], got[1][c][1]], axis=0))
                w_ref[k, pl.ds(to, 16), sl] = a_hi
                w_ref[k, pl.ds(to + rank, 16), sl] = b_hi
                w_ref[k, pl.ds(to + 2 * rank, 16), sl] = a_lo
                w_ref[k, pl.ds(to + 3 * rank, 16), sl] = b_lo
            return 0

        lax.fori_loop(0, half // 16, fill, 0)

    lane = lax.broadcasted_iota(jnp.int32, (rank, steps), 1)
    row8 = lax.broadcasted_iota(jnp.int32, (8, TILE), 0)

    def residual(w, reac, init, src, src_next):
        lin = dot(qt_ref[...], w[0 : 4 * rank], 1, 0)
        u = dot(qt_ref[:, 0:rank], w[4 * rank : 5 * rank], 1, 0)
        ru2 = reac * (u * u)
        full = lin + ru2 * u
        res = full[0:steps] - src
        res = jnp.concatenate([res[0:8] - jnp.where(row8 == 0, init, 0.0), res[8:]], axis=0)
        after = full[steps : steps + 1] - src_next
        return res, after, ru2[0:steps]

    acc1_ref[...] = jnp.zeros_like(acc1_ref)
    acc2_ref[...] = jnp.zeros_like(acc2_ref)
    acc3_ref[...] = jnp.zeros_like(acc3_ref)
    live = flag_ref[1]

    y_ref[...] = jnp.zeros_like(y_ref)
    sn_ref[...] = srcn_ref[0 : nodes // 128, :]

    def tile(n, _):
        here = pl.ds(pl.multiple_of(n * TILE, TILE), TILE)
        w = w_ref[n]
        src = jnp.transpose(src_ref[here, :]).astype(F32)
        src_next = jnp.concatenate([sn_ref[pl.ds(2 * n, 1), :], sn_ref[pl.ds(2 * n + 1, 1), :]], axis=1)
        res, after, ru2 = residual(w, row_ref[n, 0:1, :], row_ref[n, 1:2, :], src, src_next)
        rn = live * after
        rn_ref[n] = jnp.broadcast_to(rn, (8, TILE))
        y_ref[...] += (w[rank : 2 * rank].astype(F32) + w[3 * rank : 4 * rank].astype(F32)) * rn
        r_hi, r_lo = halves(res)
        c_hi, c_lo = halves(3.0 * ru2 * res)
        acc1_ref[...] += dot(w[0 : 4 * rank], r_hi, 1, 1)
        acc2_ref[...] += dot(w[0 : 2 * rank], r_lo, 1, 1)
        s = w[4 * rank : 5 * rank]
        acc3_ref[...] += dot(
            jnp.concatenate([s, s], axis=1), jnp.concatenate([c_hi, c_lo], axis=1), 1, 1
        )
        g_ref[n, 0 : 2 * rank, :] = dot(tt_ref[...], jnp.concatenate([r_hi, r_lo], axis=0), 1, 0)
        g_ref[n, 2 * rank : 3 * rank, :] = dot(tt_ref[0:rank, :], jnp.concatenate([c_hi, c_lo], axis=0), 1, 0)
        return 0

    lax.fori_loop(0, nodes // TILE, tile, 0, unroll=UNROLL)

    n_edge = nodes // TILE
    src = jnp.transpose(edge_ref[...]).astype(F32)
    res, _, _ = residual(w_ref[n_edge], row_ref[n_edge, 0:1, :], row_ref[n_edge, 1:2, :], src, 0.0)
    r_hi, r_lo = halves(res)
    g_ref[n_edge, 0:rank, :] = dot(tt_ref[0:rank, :], jnp.concatenate([r_hi, r_lo], axis=0), 1, 0)

    y_next = jnp.sum(y_ref[...], axis=1, keepdims=True)

    for base, ref in ((0, gs_own_ref), (half, gs_oth_ref)):
        def finish(i, _, base=base, ref=ref):
            at = pl.multiple_of(i * 8, 8)
            to = pl.multiple_of(base + i * 8, 8)
            tl = tlast_ref[pl.ds(to, 8), :]

            def keep(c, value, v):
                if c in (0, n_tile - 1):
                    return
                sl = slice(c * PAD, (c + 1) * PAD)
                here = slice((c - 1) * PAD, c * PAD)
                m = band_ref[8 * (2 * W + 1) : 8 * (2 * W + 2), sl]
                k, lanes = place(c)
                g2 = g_ref[k, pl.ds(to + rank, 8), lanes]
                g3 = g_ref[k, pl.ds(to + 2 * rank, 8), lanes]
                ref[pl.ds(at, 8), here] = value - m * (g2 + tl * rn_ref[k, :, lanes]) + g3

            at_tile = [place(c) for c in range(n_tile)]
            banded([g_ref[k, pl.ds(to, 8), lanes] for k, lanes in at_tile], keep)
            return 0

        lax.fori_loop(0, half // 8, finish, 0)

    zb = acc1_ref[rank : 2 * rank, :] + acc1_ref[3 * rank : 4 * rank, :] + acc2_ref[rank : 2 * rank, :]
    za = acc1_ref[0:rank, :] + acc1_ref[2 * rank : 3 * rank, :] + acc2_ref[0:rank, :] + acc3_ref[...]
    shifted = pltpu.roll(zb, steps - 1, 1)
    gt_ref[...] = za - jnp.where(lane == steps - 1, y_next, shifted)


def body(space_factor, time_factor, initial_state, link, conductivity, mass, reaction, source):
    own_rank, nodes = space_factor.shape
    time_rank, steps = time_factor.shape
    n_space = lax.axis_size("space")
    n_tm = lax.axis_size("tm")
    n_z = n_tm // 2
    rank = own_rank * n_tm
    ext = nodes + 2 * PAD
    t_id = lax.axis_index("tm")
    x_id = t_id % 2
    z_groups = [[2 * z + x for z in range(n_z)] for x in range(2)]
    pair = [(i, i ^ 1) for i in range(n_tm)]
    as_row = lambda a: a.reshape(1, nodes)
    coefs = [as_row(conductivity), as_row(link), as_row(mass), as_row(reaction), as_row(initial_state)]

    ends = []
    specs = []
    n_end = nodes // PAD - 1
    for a in [space_factor] + coefs:
        ends += [a, a]
        specs += [
            pl.BlockSpec((a.shape[0], PAD), lambda i: (0, 0)),
            pl.BlockSpec((a.shape[0], PAD), lambda i: (0, n_end)),
        ]
    ends += [source, source, source, time_factor]
    specs += [
        pl.BlockSpec((16, steps), lambda i: (0, 0)),
        pl.BlockSpec((16, steps), lambda i: (nodes // 16 - 1, 0)),
        pl.BlockSpec((nodes, PAD), lambda i: (0, 0)),
        pl.BlockSpec((time_rank, steps), lambda i: (0, 0)),
    ]
    n_row = nodes // PAD
    to_up, to_down, to_prev, to_next = pl.pallas_call(
        pack_kernel,
        grid=(1,),
        in_specs=specs,
        out_specs=[pl.BlockSpec((n, PAD), lambda i: (0, 0)) for n in (16, 16, n_row + 8, 8)],
        out_shape=[jax.ShapeDtypeStruct((n, PAD), F32) for n in (16, 16, n_row + 8, 8)],
        name="pack_ends",
    )(*ends)
    below = lax.ppermute(to_up, "space", [(i, i + 1) for i in range(n_space - 1)])
    above = lax.ppermute(to_down, "space", [(i, i - 1) for i in range(1, n_space)])
    after = lax.ppermute(to_prev, "tm", [(i, i - 1) for i in range(1, n_tm)])
    before = lax.ppermute(to_next, "tm", [(i, i + 1) for i in range(n_tm - 1)])

    s_ext = jnp.concatenate([below[0:own_rank].astype(BF), space_factor, above[0:own_rank].astype(BF)], axis=1)
    s_own = lax.all_to_all(
        jnp.broadcast_to(s_ext[None], (n_z, own_rank, ext)), "tm", 0, 0,
        axis_index_groups=z_groups, tiled=True,
    ).reshape(rank // 2, ext)
    s_own, below, above, after, before, time_factor = lax.optimization_barrier(
        (s_own, below, above, after, before, time_factor)
    )
    s_oth = lax.ppermute(s_own, "tm", pair)

    def turn(a):
        return jnp.where(x_id == 0, a, jnp.concatenate([a[own_rank:], a[:own_rank]], axis=0))

    beside = jnp.concatenate(
        [turn(after[n_row, :time_rank]), turn(before[1, :time_rank]), jnp.zeros((PAD - 2 * time_rank,), F32)]
    ).astype(BF)
    turned = turn(time_factor)
    chunk = jnp.concatenate([turned[:, :PAD], turned[:, PAD:], beside[None], jnp.zeros((7, PAD), BF)], axis=0)

    def open_src(block):
        return jnp.concatenate([block[8:12], block[12:16]], axis=1).astype(BF)

    zero = jnp.zeros((PAD - 4, steps), BF)
    edge = jnp.concatenate([zero, open_src(below), open_src(above), zero], axis=0)
    chunk, edge = lax.optimization_barrier((chunk, edge))
    in1 = lax.all_to_all(
        jnp.broadcast_to(chunk[None], (n_space,) + chunk.shape), "space", 0, 0, tiled=True
    )

    def by_half(a):
        a = a.reshape((n_z, 2, own_rank) + a.shape[2:])
        return jnp.concatenate([a[:, 0], a[:, 1]], axis=0).reshape((rank,) + a.shape[3:])

    t_perm = jnp.concatenate([by_half(in1[:, 0:time_rank]), by_half(in1[:, time_rank : 2 * time_rank])], axis=1)
    t_next = by_half(in1[:, 2 * time_rank, 0:time_rank])
    t_prev = by_half(in1[:, 2 * time_rank, time_rank : 2 * time_rank])
    t_last = t_perm[:, -1]
    tsh = jnp.concatenate([t_prev[:, None], t_perm[:, :-1]], axis=1)
    now = jnp.concatenate([t_perm, t_next[:, None], jnp.zeros((rank, 15), BF)], axis=1).T
    ago = jnp.concatenate([tsh, t_last[:, None], jnp.zeros((rank, 15), BF)], axis=1).T
    qt = jnp.concatenate([now, -ago, now, -ago], axis=1)
    tsh0 = jnp.concatenate([jnp.zeros((rank, 1), BF), t_perm[:, :-1]], axis=1)
    tt = jnp.concatenate([t_perm, tsh0], axis=0)
    tt = jnp.concatenate([tt, tt], axis=1)
    t_last = jnp.broadcast_to(t_last.astype(F32)[:, None], (rank, 128))
    flags = jnp.stack([jnp.where(t_id == 0, 1.0, 0.0), jnp.where(t_id == n_tm - 1, 0.0, 1.0)])

    vmem = pl.BlockSpec(memory_space=pltpu.VMEM)
    gs_own, gs_oth, gt = pl.pallas_call(
        compute_kernel,
        in_specs=[pl.BlockSpec(memory_space=pltpu.SMEM)] + [vmem] * 15,
        out_shape=(
            jax.ShapeDtypeStruct((rank // 2, nodes), F32),
            jax.ShapeDtypeStruct((rank // 2, nodes), F32),
            jax.ShapeDtypeStruct((rank, steps), F32),
        ),
        scratch_shapes=[
            pltpu.VMEM((ext // TILE, 5 * rank, TILE), BF),
            pltpu.VMEM((ext // TILE, 3 * rank, TILE), F32),
            pltpu.VMEM((8, ext), F32),
            pltpu.VMEM((8 * (2 * W + 2), ext), F32),
            pltpu.VMEM((ext // TILE, 8, TILE), F32),
            pltpu.VMEM((nodes // 128, 128), F32),
            pltpu.VMEM((ext // TILE, 8, TILE), F32),
            pltpu.VMEM((rank, TILE), F32),
            pltpu.VMEM((4 * rank, steps), F32),
            pltpu.VMEM((2 * rank, steps), F32),
            pltpu.VMEM((rank, steps), F32),
        ],
        compiler_params=pltpu.CompilerParams(vmem_limit_bytes=48 * 1024 * 1024),
        name="residual_gradient",
    )(flags, s_own, s_oth, tt, qt, t_last, below, above, *coefs, after, source, edge)

    came = lax.ppermute(gs_oth, "tm", pair)
    gt = gt.reshape(2, n_space, own_rank, steps).transpose(1, 0, 2, 3).reshape(n_space, time_rank, steps)
    gt_in = lax.all_to_all(gt, "space", 0, 0, tiled=True)
    chunk_rows = own_rank * n_row + 8
    part = pl.pallas_call(
        encode_kernel,
        out_shape=jax.ShapeDtypeStruct((n_z, chunk_rows, PAD), jnp.int16),
        scratch_shapes=[pltpu.VMEM(((rank // 2) * n_row + 8 * n_z, PAD), F32)],
        name="encode_sums",
    )(gs_own, came)
    part = lax.all_to_all(part, "tm", 0, 0, axis_index_groups=z_groups, tiled=True)
    part, gt_in = lax.optimization_barrier((part, gt_in))
    grad_space = pl.pallas_call(
        functools.partial(decode_kernel, 1.0 / math.sqrt(steps * n_tm)),
        out_shape=jax.ShapeDtypeStruct((own_rank, nodes), F32),
        name="decode_sums",
    )(part)

    gt = jnp.sum(gt_in, axis=0)
    swapped = jnp.concatenate([gt[own_rank:], gt[:own_rank]], axis=0)
    grad_time = jnp.where(x_id == 0, gt, swapped) * (1.0 / math.sqrt(nodes * n_space))
    return grad_space, grad_time


def solution(mesh):
    in_specs = (
        P("tm", "space"), P("space", "tm"), P("space"), P("space"),
        P("space"), P("space"), P("space"), P("space", "tm"),
    )
    out_specs = (P("tm", "space"), P("space", "tm"))

    return jax.shard_map(body, mesh=mesh, in_specs=in_specs, out_specs=out_specs, check_vma=False)
```

```python
import functools
import math

import jax
import jax.numpy as jnp
from jax import lax
from jax.experimental import pallas as pl
from jax.experimental.pallas import tpu as pltpu
from jax.sharding import PartitionSpec as P


W = 4
PAD = 128
TILE = 256
UNROLL = 4
BF = jnp.bfloat16
F32 = jnp.float32


def dot(a, b, ca, cb):
    return lax.dot_general(a, b, (((ca,), (cb,)), ((), ())), preferred_element_type=F32)


def halves(x):
    hi = x.astype(BF)
    return hi, (x - hi.astype(F32)).astype(BF)


def pack_kernel(
    s_lo, s_hi, cond_lo, cond_hi, link_lo, link_hi, mass_lo, mass_hi, reac_lo, reac_hi,
    init_lo, init_hi, src_lo, src_hi, src_first, time_ref, up_ref, down_ref, prev_ref, next_ref,
):
    for ref, parts, src in (
        (down_ref, (s_lo, cond_lo, link_lo, mass_lo, reac_lo, init_lo), src_lo[0:4, :]),
        (up_ref, (s_hi, cond_hi, link_hi, mass_hi, reac_hi, init_hi), src_hi[12:16, :]),
    ):
        rows = [p[...].astype(F32) for p in parts]
        rows.append(jnp.zeros((1, PAD), F32))
        src = src.astype(F32)
        ref[...] = jnp.concatenate(rows + [src[:, 0:PAD], src[:, PAD:]], axis=0)

    nodes = src_first.shape[0]
    steps = time_ref.shape[1]
    row = lax.broadcasted_iota(jnp.int32, (16, steps), 0)
    col = lax.broadcasted_iota(jnp.int32, (16, steps), 1)
    pick = jnp.where(((row == 0) & (col == 0)) | ((row == 1) & (col == steps - 1)), 1.0, 0.0).astype(BF)
    column = dot(pick[:, 0:PAD], src_first[...], 1, 1)
    for c in range(nodes // PAD):
        prev_ref[c : c + 1, :] = column[0:1, c * PAD : (c + 1) * PAD]
    ends = dot(pick, time_ref[...], 1, 1)[0:8]
    ends = jnp.concatenate([ends, jnp.zeros((8, PAD - ends.shape[1]), F32)], axis=1)
    prev_ref[nodes // PAD :, :] = ends
    next_ref[...] = ends


def power_of(v):
    top = jnp.max(jnp.abs(v), axis=1, keepdims=True)
    return jnp.ceil(jnp.log2(jnp.maximum(top, 1e-30)) + 0.01) - 15.0


def encode_kernel(own_ref, came_ref, out_ref, flat_ref):
    rows, nodes = own_ref.shape
    n_row = nodes // PAD
    n_z = out_ref.shape[0]
    own_rank = rows // n_z
    body = own_rank * n_row
    for g in range(rows // 8):
        step = jnp.exp2(came_ref[8 * g : 8 * g + 8, nodes:].astype(jnp.int32).astype(F32))[:, 0:1]
        v = own_ref[8 * g : 8 * g + 8, :]
        v = v + came_ref[8 * g : 8 * g + 8, 0:nodes].astype(jnp.int32).astype(F32) * step
        power = power_of(v)
        q = jnp.floor(v * jnp.exp2(-power) + 0.5)
        for c in range(n_row):
            flat_ref[pl.ds(8 * g * n_row + c, 8, stride=n_row), :] = q[:, c * PAD : (c + 1) * PAD]
        for b in range(8):
            z, at = divmod(8 * g + b, own_rank)
            flat_ref[rows * n_row + 8 * z + at : rows * n_row + 8 * z + at + 1, :] = jnp.broadcast_to(
                power[b : b + 1], (1, PAD)
            )
    for z in range(n_z):
        out_ref[z, 0:body, :] = flat_ref[z * body : (z + 1) * body, :].astype(jnp.int32).astype(jnp.int16)
        tail = flat_ref[rows * n_row + 8 * z : rows * n_row + 8 * z + 8, :]
        tail = jnp.where(lax.broadcasted_iota(jnp.int32, (8, PAD), 0) < own_rank, tail, 0.0)
        out_ref[z, body : body + 8, :] = tail.astype(jnp.int32).astype(jnp.int16)


def decode_kernel(factor, in_ref, out_ref):
    n_z = in_ref.shape[0]
    own_rank, nodes = out_ref.shape
    n_row = nodes // PAD
    body = own_rank * n_row
    total = jnp.zeros((body, PAD), F32)
    for z in range(n_z):
        step = jnp.exp2(in_ref[z, body : body + 8, :].astype(jnp.int32).astype(F32))
        q = in_ref[z, 0:body, :].astype(jnp.int32).astype(F32)
        total = total + jnp.concatenate(
            [q[b * n_row : (b + 1) * n_row] * step[b : b + 1] for b in range(own_rank)], axis=0
        )
    total = total * factor
    for b in range(own_rank):
        for c in range(n_row):
            out_ref[b : b + 1, c * PAD : (c + 1) * PAD] = total[b * n_row + c : b * n_row + c + 1]


def compute_kernel(
    flag_ref, sown_ref, soth_ref, tt_ref, qt_ref, tlast_ref,
    below_ref, above_ref, cond_ref, link_ref, mass_ref, reac_ref, init_ref, srcn_ref, src_ref, edge_ref,
    gs_own_ref, gs_oth_ref, gt_ref,
    w_ref, g_ref, coef_ref, band_ref, row_ref, sn_ref, rn_ref, y_ref, st_ref, acc1_ref, acc2_ref, acc3_ref,
):
    ext = coef_ref.shape[1]
    nodes = ext - 2 * PAD
    rank = tlast_ref.shape[0]
    half = rank // 2
    steps = src_ref.shape[1]
    main = pl.ds(PAD, nodes)
    right = pl.ds(PAD + nodes, PAD)

    for r, ref in enumerate((cond_ref, link_ref, mass_ref, reac_ref, init_ref)):
        coef_ref[r : r + 1, 0:PAD] = below_ref[2 + r : 3 + r, :]
        coef_ref[r : r + 1, main] = ref[...].astype(F32)
        coef_ref[r : r + 1, right] = above_ref[2 + r : 3 + r, :]

    cond = coef_ref[0:1, :]
    link = coef_ref[1:2, :]
    mass = coef_ref[2:3, :]
    diag = mass + cond
    tall = (8, ext)
    for d in range(1, W + 1):
        up = jnp.where(link == float(d), cond, 0.0)
        down = pltpu.roll(up, d, 1)
        band_ref[8 * d : 8 * d + 8, :] = jnp.broadcast_to(up, tall)
        band_ref[8 * (W + d) : 8 * (W + d) + 8, :] = jnp.broadcast_to(down, tall)
        diag = diag + down
    band_ref[0:8, :] = jnp.broadcast_to(diag, tall)
    band_ref[8 * (2 * W + 1) : 8 * (2 * W + 2), :] = jnp.broadcast_to(mass, tall)
    start = flag_ref[0]
    coef_ref[4:5, :] = coef_ref[4:5, :] * mass * start

    n_tile = ext // PAD

    def place(c):
        k, h = (n_tile // 2 - 1, int(c > 0)) if c in (0, n_tile - 1) else divmod(c - 1, 2)
        return k, slice(h * PAD, (h + 1) * PAD)

    for c in range(n_tile):
        k, sl = place(c)
        row_ref[k, 0:2, sl] = coef_ref[3:5, c * PAD : (c + 1) * PAD]

    lane1 = lax.broadcasted_iota(jnp.int32, (8, PAD), 1)

    def banded(tiles, keep):
        fwd = [[pltpu.roll(x, PAD - d, 1) for d in range(1, W + 1)] for x in tiles]
        bwd = [[pltpu.roll(x, d, 1) for d in range(1, W + 1)] for x in tiles]
        for c in range(n_tile):
            sl = slice(c * PAD, (c + 1) * PAD)
            nxt, prv = min(c + 1, n_tile - 1), max(c - 1, 0)
            total = band_ref[0:8, sl] * tiles[c]
            for d in range(1, W + 1):
                ahead = jnp.where(lane1 >= PAD - d, fwd[nxt][d - 1], fwd[c][d - 1])
                back = jnp.where(lane1 < d, bwd[prv][d - 1], bwd[c][d - 1])
                total = total - band_ref[8 * d : 8 * d + 8, sl] * ahead
                total = total - band_ref[8 * (W + d) : 8 * (W + d) + 8, sl] * back
            keep(c, total, tiles[c])

    for base, ref in ((0, sown_ref), (half, soth_ref)):
        def fill(i, _, base=base, ref=ref):
            at = pl.multiple_of(i * 16, 16)
            to = pl.multiple_of(base + i * 16, 16)
            s_b = ref[pl.ds(at, 16), :]
            s_f = s_b.astype(F32)
            got = []
            for h in range(2):
                mine = {}

                def keep(c, value, v, mine=mine):
                    m = band_ref[8 * (2 * W + 1) : 8 * (2 * W + 2), c * PAD : (c + 1) * PAD]
                    if c in (0, n_tile - 1):
                        value = jnp.where(m > 0.0, value, 0.0)
                    mine[c] = (value, m * v)

                banded([s_f[8 * h : 8 * h + 8, c * PAD : (c + 1) * PAD] for c in range(n_tile)], keep)
                got.append(mine)
            for c in range(n_tile):
                k, sl = place(c)
                w_ref[k, pl.ds(to + 4 * rank, 16), sl] = s_b[:, c * PAD : (c + 1) * PAD]
                a_hi, a_lo = halves(jnp.concatenate([got[0][c][0], got[1][c][0]], axis=0))
                b_hi, b_lo = halves(jnp.concatenate([got[0][c][1], got[1][c][1]], axis=0))
                w_ref[k, pl.ds(to, 16), sl] = a_hi
                w_ref[k, pl.ds(to + rank, 16), sl] = b_hi
                w_ref[k, pl.ds(to + 2 * rank, 16), sl] = a_lo
                w_ref[k, pl.ds(to + 3 * rank, 16), sl] = b_lo
            return 0

        lax.fori_loop(0, half // 16, fill, 0)

    lane = lax.broadcasted_iota(jnp.int32, (rank, steps), 1)
    row8 = lax.broadcasted_iota(jnp.int32, (8, TILE), 0)

    def residual(w, reac, init, src, src_next):
        lin = dot(qt_ref[...], w[0 : 4 * rank], 1, 0)
        u = dot(qt_ref[:, 0:rank], w[4 * rank : 5 * rank], 1, 0)
        ru2 = reac * (u * u)
        full = lin + ru2 * u
        res = full[0:steps] - src
        res = jnp.concatenate([res[0:8] - jnp.where(row8 == 0, init, 0.0), res[8:]], axis=0)
        after = full[steps : steps + 1] - src_next
        return res, after, ru2[0:steps]

    acc1_ref[...] = jnp.zeros_like(acc1_ref)
    acc2_ref[...] = jnp.zeros_like(acc2_ref)
    acc3_ref[...] = jnp.zeros_like(acc3_ref)
    live = flag_ref[1]

    y_ref[...] = jnp.zeros_like(y_ref)
    sn_ref[...] = srcn_ref[0 : nodes // 128, :]

    def tile(n, _):
        here = pl.ds(pl.multiple_of(n * TILE, TILE), TILE)
        w = w_ref[n]
        src = jnp.transpose(src_ref[here, :]).astype(F32)
        src_next = jnp.concatenate([sn_ref[pl.ds(2 * n, 1), :], sn_ref[pl.ds(2 * n + 1, 1), :]], axis=1)
        res, after, ru2 = residual(w, row_ref[n, 0:1, :], row_ref[n, 1:2, :], src, src_next)
        rn = live * after
        rn_ref[n] = jnp.broadcast_to(rn, (8, TILE))
        y_ref[...] += (w[rank : 2 * rank].astype(F32) + w[3 * rank : 4 * rank].astype(F32)) * rn
        r_hi, r_lo = halves(res)
        c_hi, c_lo = halves(3.0 * ru2 * res)
        acc1_ref[...] += dot(w[0 : 4 * rank], r_hi, 1, 1)
        acc2_ref[...] += dot(w[0 : 2 * rank], r_lo, 1, 1)
        s = w[4 * rank : 5 * rank]
        acc3_ref[...] += dot(
            jnp.concatenate([s, s], axis=1), jnp.concatenate([c_hi, c_lo], axis=1), 1, 1
        )
        g_ref[n, 0 : 2 * rank, :] = dot(tt_ref[...], jnp.concatenate([r_hi, r_lo], axis=0), 1, 0)
        g_ref[n, 2 * rank : 3 * rank, :] = dot(tt_ref[0:rank, :], jnp.concatenate([c_hi, c_lo], axis=0), 1, 0)
        return 0

    lax.fori_loop(0, nodes // TILE, tile, 0, unroll=UNROLL)

    n_edge = nodes // TILE
    src = jnp.transpose(edge_ref[...]).astype(F32)
    res, _, _ = residual(w_ref[n_edge], row_ref[n_edge, 0:1, :], row_ref[n_edge, 1:2, :], src, 0.0)
    r_hi, r_lo = halves(res)
    g_ref[n_edge, 0:rank, :] = dot(tt_ref[0:rank, :], jnp.concatenate([r_hi, r_lo], axis=0), 1, 0)

    y_next = jnp.sum(y_ref[...], axis=1, keepdims=True)

    for base, ref in ((0, gs_own_ref), (half, gs_oth_ref)):
        def finish(i, _, base=base, ref=ref):
            at = pl.multiple_of(i * 8, 8)
            to = pl.multiple_of(base + i * 8, 8)
            tl = tlast_ref[pl.ds(to, 8), :]

            def keep(c, value, v):
                if c in (0, n_tile - 1):
                    return
                sl = slice(c * PAD, (c + 1) * PAD)
                here = slice((c - 1) * PAD, c * PAD)
                m = band_ref[8 * (2 * W + 1) : 8 * (2 * W + 2), sl]
                k, lanes = place(c)
                g2 = g_ref[k, pl.ds(to + rank, 8), lanes]
                g3 = g_ref[k, pl.ds(to + 2 * rank, 8), lanes]
                value = value - m * (g2 + tl * rn_ref[k, :, lanes]) + g3
                if base:
                    st_ref[:, here] = value
                else:
                    ref[pl.ds(at, 8), here] = value

            at_tile = [place(c) for c in range(n_tile)]
            banded([g_ref[k, pl.ds(to, 8), lanes] for k, lanes in at_tile], keep)
            if base:
                v = st_ref[...]
                power = power_of(v)
                q = jnp.floor(v * jnp.exp2(-power) + 0.5)
                ref[pl.ds(at, 8), 0:nodes] = q.astype(jnp.int32).astype(jnp.int16)
                ref[pl.ds(at, 8), nodes:] = jnp.broadcast_to(power, (8, PAD)).astype(jnp.int32).astype(jnp.int16)
            return 0

        lax.fori_loop(0, half // 8, finish, 0)

    zb = acc1_ref[rank : 2 * rank, :] + acc1_ref[3 * rank : 4 * rank, :] + acc2_ref[rank : 2 * rank, :]
    za = acc1_ref[0:rank, :] + acc1_ref[2 * rank : 3 * rank, :] + acc2_ref[0:rank, :] + acc3_ref[...]
    shifted = pltpu.roll(zb, steps - 1, 1)
    gt_ref[...] = za - jnp.where(lane == steps - 1, y_next, shifted)


def body(space_factor, time_factor, initial_state, link, conductivity, mass, reaction, source):
    own_rank, nodes = space_factor.shape
    time_rank, steps = time_factor.shape
    n_space = lax.axis_size("space")
    n_tm = lax.axis_size("tm")
    n_z = n_tm // 2
    rank = own_rank * n_tm
    ext = nodes + 2 * PAD
    t_id = lax.axis_index("tm")
    x_id = t_id % 2
    z_groups = [[2 * z + x for z in range(n_z)] for x in range(2)]
    pair = [(i, i ^ 1) for i in range(n_tm)]
    as_row = lambda a: a.reshape(1, nodes)
    coefs = [as_row(conductivity), as_row(link), as_row(mass), as_row(reaction), as_row(initial_state)]

    ends = []
    specs = []
    n_end = nodes // PAD - 1
    for a in [space_factor] + coefs:
        ends += [a, a]
        specs += [
            pl.BlockSpec((a.shape[0], PAD), lambda i: (0, 0)),
            pl.BlockSpec((a.shape[0], PAD), lambda i: (0, n_end)),
        ]
    ends += [source, source, source, time_factor]
    specs += [
        pl.BlockSpec((16, steps), lambda i: (0, 0)),
        pl.BlockSpec((16, steps), lambda i: (nodes // 16 - 1, 0)),
        pl.BlockSpec((nodes, PAD), lambda i: (0, 0)),
        pl.BlockSpec((time_rank, steps), lambda i: (0, 0)),
    ]
    n_row = nodes // PAD
    to_up, to_down, to_prev, to_next = pl.pallas_call(
        pack_kernel,
        grid=(1,),
        in_specs=specs,
        out_specs=[pl.BlockSpec((n, PAD), lambda i: (0, 0)) for n in (16, 16, n_row + 8, 8)],
        out_shape=[jax.ShapeDtypeStruct((n, PAD), F32) for n in (16, 16, n_row + 8, 8)],
        name="pack_ends",
    )(*ends)
    below = lax.ppermute(to_up, "space", [(i, i + 1) for i in range(n_space - 1)])
    above = lax.ppermute(to_down, "space", [(i, i - 1) for i in range(1, n_space)])
    after = lax.ppermute(to_prev, "tm", [(i, i - 1) for i in range(1, n_tm)])
    before = lax.ppermute(to_next, "tm", [(i, i + 1) for i in range(n_tm - 1)])

    s_ext = jnp.concatenate([below[0:own_rank].astype(BF), space_factor, above[0:own_rank].astype(BF)], axis=1)
    s_own = lax.all_to_all(
        jnp.broadcast_to(s_ext[None], (n_z, own_rank, ext)), "tm", 0, 0,
        axis_index_groups=z_groups, tiled=True,
    ).reshape(rank // 2, ext)
    s_own, below, above, after, before, time_factor = lax.optimization_barrier(
        (s_own, below, above, after, before, time_factor)
    )
    s_oth = lax.ppermute(s_own, "tm", pair)

    def turn(a):
        return jnp.where(x_id == 0, a, jnp.concatenate([a[own_rank:], a[:own_rank]], axis=0))

    beside = jnp.concatenate(
        [turn(after[n_row, :time_rank]), turn(before[1, :time_rank]), jnp.zeros((PAD - 2 * time_rank,), F32)]
    ).astype(BF)
    turned = turn(time_factor)
    chunk = jnp.concatenate([turned[:, :PAD], turned[:, PAD:], beside[None], jnp.zeros((7, PAD), BF)], axis=0)

    def open_src(block):
        return jnp.concatenate([block[8:12], block[12:16]], axis=1).astype(BF)

    zero = jnp.zeros((PAD - 4, steps), BF)
    edge = jnp.concatenate([zero, open_src(below), open_src(above), zero], axis=0)
    chunk, edge = lax.optimization_barrier((chunk, edge))
    in1 = lax.all_to_all(
        jnp.broadcast_to(chunk[None], (n_space,) + chunk.shape), "space", 0, 0, tiled=True
    )

    def by_half(a):
        a = a.reshape((n_z, 2, own_rank) + a.shape[2:])
        return jnp.concatenate([a[:, 0], a[:, 1]], axis=0).reshape((rank,) + a.shape[3:])

    t_perm = jnp.concatenate([by_half(in1[:, 0:time_rank]), by_half(in1[:, time_rank : 2 * time_rank])], axis=1)
    t_next = by_half(in1[:, 2 * time_rank, 0:time_rank])
    t_prev = by_half(in1[:, 2 * time_rank, time_rank : 2 * time_rank])
    t_last = t_perm[:, -1]
    tsh = jnp.concatenate([t_prev[:, None], t_perm[:, :-1]], axis=1)
    now = jnp.concatenate([t_perm, t_next[:, None], jnp.zeros((rank, 15), BF)], axis=1).T
    ago = jnp.concatenate([tsh, t_last[:, None], jnp.zeros((rank, 15), BF)], axis=1).T
    qt = jnp.concatenate([now, -ago, now, -ago], axis=1)
    tsh0 = jnp.concatenate([jnp.zeros((rank, 1), BF), t_perm[:, :-1]], axis=1)
    tt = jnp.concatenate([t_perm, tsh0], axis=0)
    tt = jnp.concatenate([tt, tt], axis=1)
    t_last = jnp.broadcast_to(t_last.astype(F32)[:, None], (rank, 128))
    flags = jnp.stack([jnp.where(t_id == 0, 1.0, 0.0), jnp.where(t_id == n_tm - 1, 0.0, 1.0)])

    vmem = pl.BlockSpec(memory_space=pltpu.VMEM)
    gs_own, gs_oth, gt = pl.pallas_call(
        compute_kernel,
        in_specs=[pl.BlockSpec(memory_space=pltpu.SMEM)] + [vmem] * 15,
        out_shape=(
            jax.ShapeDtypeStruct((rank // 2, nodes), F32),
            jax.ShapeDtypeStruct((rank // 2, nodes + PAD), jnp.int16),
            jax.ShapeDtypeStruct((rank, steps), F32),
        ),
        scratch_shapes=[
            pltpu.VMEM((ext // TILE, 5 * rank, TILE), BF),
            pltpu.VMEM((ext // TILE, 3 * rank, TILE), F32),
            pltpu.VMEM((8, ext), F32),
            pltpu.VMEM((8 * (2 * W + 2), ext), F32),
            pltpu.VMEM((ext // TILE, 8, TILE), F32),
            pltpu.VMEM((nodes // 128, 128), F32),
            pltpu.VMEM((ext // TILE, 8, TILE), F32),
            pltpu.VMEM((rank, TILE), F32),
            pltpu.VMEM((8, nodes), F32),
            pltpu.VMEM((4 * rank, steps), F32),
            pltpu.VMEM((2 * rank, steps), F32),
            pltpu.VMEM((rank, steps), F32),
        ],
        compiler_params=pltpu.CompilerParams(vmem_limit_bytes=48 * 1024 * 1024),
        name="residual_gradient",
    )(flags, s_own, s_oth, tt, qt, t_last, below, above, *coefs, after, source, edge)

    came = lax.ppermute(gs_oth, "tm", pair)
    gt = gt.reshape(2, n_space, own_rank, steps).transpose(1, 0, 2, 3).reshape(n_space, time_rank, steps)
    gt_in = lax.all_to_all(gt, "space", 0, 0, tiled=True)
    chunk_rows = own_rank * n_row + 8
    part = pl.pallas_call(
        encode_kernel,
        out_shape=jax.ShapeDtypeStruct((n_z, chunk_rows, PAD), jnp.int16),
        scratch_shapes=[pltpu.VMEM(((rank // 2) * n_row + 8 * n_z, PAD), F32)],
        name="encode_sums",
    )(gs_own, came)
    part = lax.all_to_all(part, "tm", 0, 0, axis_index_groups=z_groups, tiled=True)
    part, gt_in = lax.optimization_barrier((part, gt_in))
    grad_space = pl.pallas_call(
        functools.partial(decode_kernel, 1.0 / math.sqrt(steps * n_tm)),
        out_shape=jax.ShapeDtypeStruct((own_rank, nodes), F32),
        name="decode_sums",
    )(part)

    gt = jnp.sum(gt_in, axis=0)
    swapped = jnp.concatenate([gt[own_rank:], gt[:own_rank]], axis=0)
    grad_time = jnp.where(x_id == 0, gt, swapped) * (1.0 / math.sqrt(nodes * n_space))
    return grad_space, grad_time


def solution(mesh):
    in_specs = (
        P("tm", "space"), P("space", "tm"), P("space"), P("space"),
        P("space"), P("space"), P("space"), P("space", "tm"),
    )
    out_specs = (P("tm", "space"), P("space", "tm"))

    return jax.shard_map(body, mesh=mesh, in_specs=in_specs, out_specs=out_specs, check_vma=False)
```
